32 devices in a mesh: img: 16 (over z, x, core), fou: 2 (over y).
Axes of the slice: x: 2, y: 2, z: 4, core: 2. Of those that a mesh axis runs over, the one named last changes fastest.
Arguments:
- sky_estimate: float32 [4, 2048, 2048], P(None, 'img', 'fou'), may hold values from 0 to 2
- dual_coeffs: bfloat16 [4, 9, 2048, 2048], P(None, None, 'img', 'fou'), may hold values from -2 to 2
- dirty_image: float32 [4, 2048, 2048], P(None, 'img', 'fou'), may hold values from -4 to 4
- filters: float32 [8, 17], replicated, may hold values from -1.5 to 1.5
- thresholds: float32 [9], replicated, may hold values from 0.2 to 1.2
- facet_rows: int32 [16], P('img'), may hold values from 32 to 128, as said below
- tile_slots: int32 [4, 32, 6], P(None, 'img'), may hold values from 0 to 31, as said below
- tile_count: int32 [4, 32], P(None, 'img'), may hold values from 1 to 6, as said below
- gram_tiles: bfloat16 [4, 32, 6, 64, 64], P(None, 'img'), may hold values from -4 to 4
Outputs:
- image_next: float32 [4, 2048, 2048], P(None, 'img', 'fou')
- dual_next: bfloat16 [4, 9, 2048, 2048], P(None, None, 'img', 'fou')
The draws below stay inside these ranges and needn't reach their ends.
Inputs may be any that keep to these rules, and one draw needn't show every extreme that they name: `facet_rows`: facet f covers image rows f * 128 to (f + 1) * 128 - 1; some facet is full. `tile_slots`: the 6 entries of one channel and v-tile are distinct. `tile_count`: slots at or beyond the count hold no tile; in each channel some v-tile uses all 6 slots.
All inputs are finite; a program needn't handle non-finite values.
Results may differ from the reference program's by a relative error of at most 0.005.
Values may be sent and summed in bfloat16 or wider, within the bound.
A program may use at most 192 MiB of HBM per device.

```python
import math
import jax
import jax.numpy as jnp
from jax import lax

PIXELS = 2048
CHANNELS = 4
FRAMES = 9
RADIUS = 8
BLOCK = 64
SLOTS = 6
BLOCKS = 32
FACETS = 16
ROWS_IMG = 128


def draw_facet_rows(key, part):
    first, second = jax.random.split(jax.random.fold_in(key, 11))
    counts = jax.random.randint(first, (FACETS,), ROWS_IMG // 4, ROWS_IMG + 1)
    chosen = jax.random.randint(second, (), 0, FACETS)
    return jnp.where(jnp.arange(FACETS) == chosen, ROWS_IMG, counts).astype(jnp.int32)


def draw_tile_slots(key, part):
    scores = jax.random.randint(jax.random.fold_in(key, 23), (CHANNELS, BLOCKS, BLOCKS), 0, 1 << 20)
    scores = scores * BLOCKS + jnp.arange(BLOCKS, dtype=jnp.int32)[None, None, :]
    ordering = jnp.argsort(scores, axis=-1)
    return ordering[:, :, :SLOTS].astype(jnp.int32)


def draw_tile_count(key, part):
    first, second = jax.random.split(jax.random.fold_in(key, 37))
    counts = jax.random.randint(first, (CHANNELS, BLOCKS), 1, SLOTS + 1)
    chosen = jax.random.randint(second, (CHANNELS, 1), 0, BLOCKS)
    return jnp.where(jnp.arange(BLOCKS)[None, :] == chosen, SLOTS, counts).astype(jnp.int32)


def draw_gram_tiles(key, part):
    first, second = jax.random.split(jax.random.fold_in(key, 53))
    shape = (CHANNELS, BLOCKS, SLOTS, BLOCK, BLOCK)
    diagonal = jax.random.uniform(first, shape[:-1], jnp.float32, 0.5, 2.0)
    noise = jax.random.normal(second, shape, jnp.float32)
    noise = (noise + jnp.swapaxes(noise, -1, -2)) * (0.5 / BLOCK ** 0.5)
    identity = jnp.eye(BLOCK, dtype=jnp.float32)
    return (noise + identity * diagonal[..., None]).astype(jnp.bfloat16)


def level_of(key, shape, cuts, smallest, high):
    def one(axis_at, shards_of):
        heights = jax.random.uniform(jax.random.fold_in(jax.random.fold_in(key, 6), axis_at), (shards_of,), jnp.float32, smallest / len(cuts), high / len(cuts))
        return jnp.repeat(jnp.exp(heights), shape[axis_at] // shards_of).reshape((-1,) + (1,) * (len(shape) - axis_at - 1))

    loudness = one(*cuts[0])
    for cut in cuts[1:]:
        loudness = loudness * one(*cut)
    return loudness


def gaussian(stream_key, dims, spread, reach, pieces=(), kind=jnp.bfloat16):
    gain = level_of(stream_key, dims, pieces, -0.22, 0.18) if pieces else 1.0
    array = jax.random.normal(stream_key, dims, jnp.float32) * spread * gain
    return jnp.minimum(jnp.maximum(array, -reach), reach).astype(kind)


def setup_inputs(seed: int = 0) -> dict:
    keys = jax.random.split(jax.random.key(seed), 10)
    sky_estimate = jnp.clip(2.0 * jax.random.uniform(keys[0], (CHANNELS, PIXELS, PIXELS), jnp.float32) ** level_of(keys[0], (CHANNELS, PIXELS, PIXELS), ((1, 16), (2, 2)), -0.2, 0.2), 0.0, 2.0)
    dual_coeffs = gaussian(keys[1], (CHANNELS, FRAMES, PIXELS, PIXELS), 0.3, 2.0, ((2, 16), (3, 2)))
    dirty_image = gaussian(keys[2], (CHANNELS, PIXELS, PIXELS), 0.5, 4.0, ((1, 16), (2, 2)), jnp.float32)
    filters = gaussian(keys[3], (FRAMES - 1, 2 * RADIUS + 1), (2 * RADIUS + 1) ** -0.5, 1.5, (), jnp.float32)
    thresholds = jnp.clip(jnp.exp(jax.random.uniform(keys[4], (FRAMES,), jnp.float32, math.log(0.2), math.log(1.2))), 0.2, 1.2)
    facet_rows = draw_facet_rows(jax.random.fold_in(keys[9], 71), 0)
    tile_slots = draw_tile_slots(jax.random.fold_in(keys[9], 71), 0)
    tile_count = draw_tile_count(jax.random.fold_in(keys[9], 71), 0)
    gram_tiles = draw_gram_tiles(jax.random.fold_in(keys[9], 71), 0)
    return dict(sky_estimate=sky_estimate, dual_coeffs=dual_coeffs, dirty_image=dirty_image, filters=filters, thresholds=thresholds, facet_rows=facet_rows, tile_slots=tile_slots, tile_count=tile_count, gram_tiles=gram_tiles)


STEP_PRIMAL = 0.5
STEP_DUAL = 0.5
PRECISE = lax.Precision.HIGHEST

def correlate(planes, filter_taps):
    groups = filter_taps.shape[0]
    radius = (filter_taps.shape[1] - 1) // 2
    layout = ('NCHW', 'OIHW', 'NCHW')
    rowwise = lax.conv_general_dilated(planes, filter_taps[:, None, :, None], (1, 1), ((radius, radius), (0, 0)), dimension_numbers=layout, feature_group_count=groups, precision=PRECISE)
    return lax.conv_general_dilated(rowwise, filter_taps[:, None, None, :], (1, 1), ((0, 0), (radius, radius)), dimension_numbers=layout, feature_group_count=groups, precision=PRECISE)

def reference(sky_estimate, dual_coeffs, dirty_image, filters, thresholds, facet_rows, tile_slots, tile_count, gram_tiles):
    taps_len = 2 * RADIUS + 1
    identity_tap = (jnp.arange(taps_len, dtype=jnp.int32) == RADIUS).astype(jnp.float32)
    all_taps = jnp.concatenate([identity_tap[None, :], filters], axis=0)
    flipped = all_taps[:, ::-1]

    def synth_channel(frames_one):
        return lax.optimization_barrier(jnp.sum(correlate(frames_one[None], flipped)[0], axis=0))
    synthesis = lax.map(synth_channel, dual_coeffs.astype(jnp.float32))
    spectrum = jnp.fft.fft2(sky_estimate)
    by_tile = jnp.swapaxes(spectrum, 1, 2).reshape(CHANNELS, BLOCKS, BLOCK, BLOCKS, BLOCK)
    positions = jnp.broadcast_to(tile_slots[:, :, None, :, None], (CHANNELS, BLOCKS, BLOCK, SLOTS, BLOCK))
    picked = jnp.take_along_axis(by_tile, positions, axis=3)
    in_use = (jnp.arange(SLOTS, dtype=jnp.int32)[None, None, :] < tile_count[:, :, None]).astype(jnp.float32)
    masked = gram_tiles.astype(jnp.float32) * in_use[:, :, :, None, None]
    selector = (tile_slots[:, :, :, None] == jnp.arange(BLOCKS, dtype=jnp.int32)[None, None, None, :]).astype(jnp.float32) * in_use[:, :, :, None]

    def weigh_part(plane_part):
        product = jnp.einsum('cqvsa,cqsab->cqvsb', plane_part, masked, precision=PRECISE)
        placed = jnp.einsum('cqvsb,cqst->cqvtb', product, selector, precision=PRECISE)
        return jnp.swapaxes(placed.reshape(CHANNELS, PIXELS, PIXELS), 1, 2)
    weighted = lax.complex(weigh_part(jnp.real(picked).astype(jnp.float32)), weigh_part(jnp.imag(picked).astype(jnp.float32)))
    gram_image = jnp.real(jnp.fft.ifft2(weighted)).astype(jnp.float32)
    counter = jnp.arange(PIXELS, dtype=jnp.int32)
    live_rows = (counter % ROWS_IMG < facet_rows[counter // ROWS_IMG]).astype(jnp.float32)
    image_next = jnp.maximum(sky_estimate - STEP_PRIMAL * (gram_image - dirty_image + synthesis), 0.0) * live_rows[None, :, None]
    probe = 2.0 * image_next - sky_estimate

    def update_frame(item):
        frame_taps, bound, current = item
        coeffs = correlate(probe[:, None], frame_taps[None, :])[:, 0]
        candidate = current.astype(jnp.float32) + STEP_DUAL * coeffs
        magnitude = jnp.sqrt(lax.optimization_barrier(jnp.sum(candidate * candidate, axis=0)))
        return (candidate * (bound / jnp.maximum(magnitude, bound))).astype(jnp.bfloat16)
    dual_next = jnp.swapaxes(lax.map(update_frame, (all_taps, thresholds, jnp.swapaxes(dual_coeffs, 0, 1))), 0, 1)
    return (image_next, dual_next)
```

```python
import functools
import math

import jax
import jax.numpy as jnp
import numpy as np
from jax import lax
from jax.experimental import pallas as pl
from jax.experimental.pallas import tpu as pltpu
from jax.sharding import PartitionSpec as P

STEP_PRIMAL = 0.5
STEP_DUAL = 0.5
LANES = 128
BF16 = jnp.bfloat16
F32 = jnp.float32


def dot(a, b, dims=((1,), (0,)), **kw):
    return lax.dot_general(a, b, (dims, ((), ())), preferred_element_type=F32, **kw)


def flip_halves(x):
    half = x.shape[-1] // 2
    return jnp.concatenate([x[:, half:], x[:, :half]], axis=1)


def half_sign(rows, lanes, dtype=F32):
    lane = lax.broadcasted_iota(jnp.int32, (rows, lanes), 1)
    return jnp.where(lane < lanes // 2, 1.0, -1.0).astype(dtype)


def tables(line, block):
    small = np.arange(block)[:, None] * np.arange(line)[None, :] % line
    angle = small * (2.0 * math.pi / line)
    by_row = np.concatenate([np.cos(angle), np.sin(angle)], axis=0).astype(np.float32)
    period = line // block
    turn = np.arange(period)[:, None] * np.arange(period)[None, :] % period
    turn = turn * (2.0 * math.pi / period)
    return by_row, np.cos(turn).astype(np.float32), np.sin(turn).astype(np.float32)


def turned(base, other, cos_tile, sin_tile):
    rows, lanes = base.shape
    period = cos_tile.shape[0]
    base = base.reshape(rows // period, period, lanes)
    other = other.reshape(rows // period, period, lanes)
    out = base * cos_tile[None] + other * sin_tile[None]
    return out.reshape(rows, lanes).astype(BF16)


def forward_kernel(x_ref, et_ref, es_ref, pc_ref, ps_ref, o_ref):
    both = [turned(et_ref[...], es_ref[...], pc_ref[i], ps_ref[i]) for i in range(2)]
    lanes = et_ref.shape[1]
    out = dot(x_ref[...], jnp.concatenate(both, axis=1))
    sign = half_sign(1, lanes)
    for i in range(2):
        o_ref[i] = (out[:, i * lanes : (i + 1) * lanes] * sign).astype(BF16)


def forward(x, et, es, pc, ps):
    rows, line = x.shape
    tiles, period, lanes = pc.shape
    whole = pl.BlockSpec((line, lanes), lambda i: (0, 0))
    turn = pl.BlockSpec((2, period, lanes), lambda i: (i, 0, 0))
    return pl.pallas_call(
        forward_kernel,
        grid=(tiles // 2,),
        in_specs=[pl.BlockSpec((rows, line), lambda i: (0, 0)), whole, whole, turn, turn],
        out_specs=pl.BlockSpec((2, rows, lanes), lambda i: (i, 0, 0)),
        out_shape=jax.ShapeDtypeStruct((tiles, rows, lanes), BF16),
        name="forward",
    )(x, et, es, pc, ps)


def backward_kernel(scale, y_ref, et_ref, es_ref, pc_ref, ps_ref, o_ref, all_y, table):
    tiles, rows, lanes = y_ref.shape

    @pl.when(pl.program_id(0) == 0)
    def _():
        sign = half_sign(1, lanes)
        for q in range(tiles):
            all_y[:, q * lanes : (q + 1) * lanes] = (y_ref[q].astype(F32) * sign).astype(BF16)

    for q in range(tiles):
        table[:, q * lanes : (q + 1) * lanes] = turned(
            et_ref[...], es_ref[...], pc_ref[q], ps_ref[q]
        )
    out = dot(all_y[...], table[...], ((1,), (1,)))
    o_ref[...] = (out * scale).astype(BF16)


def backward(y, et, es, pc, ps, scale):
    tiles, rows, lanes = y.shape
    line = et.shape[0]
    part = min(256, line)
    chunk = pl.BlockSpec((part, lanes), lambda i: (i, 0))
    fixed = pl.BlockSpec(pc.shape, lambda i: (0, 0, 0))
    return pl.pallas_call(
        functools.partial(backward_kernel, scale),
        grid=(line // part,),
        in_specs=[pl.BlockSpec((tiles, rows, lanes), lambda i: (0, 0, 0)), chunk, chunk, fixed, fixed],
        out_specs=pl.BlockSpec((rows, part), lambda i: (0, i)),
        out_shape=jax.ShapeDtypeStruct((rows, line), BF16),
        scratch_shapes=[
            pltpu.VMEM((rows, tiles * lanes), BF16),
            pltpu.VMEM((part, tiles * lanes), BF16),
        ],
        name="backward",
    )(y, et, es, pc, ps)


def gram_kernel(slots_ref, x_ref, g_ref, e_ref, et_ref, es_ref, rc_ref, rs_ref, pc_ref, ps_ref,
                o_ref, table, table_t):
    c = pl.program_id(0)
    parts, _, rows, lanes = x_ref.shape
    wide, line = e_ref.shape
    block = wide // 2
    slots = g_ref.shape[1]
    x = x_ref[:, 0].reshape(parts * rows, lanes)
    top, low = e_ref[:block], e_ref[block:]
    for k in range(slots):
        t = slots_ref[c, k]
        cos_row = rc_ref[pl.ds(t, 1), :]
        sin_row = rs_ref[pl.ds(t, 1), :]
        table[k * wide : k * wide + block] = (top * cos_row - low * sin_row).astype(BF16)
        table[k * wide + block : (k + 1) * wide] = (low * cos_row + top * sin_row).astype(BF16)
        table_t[:, k * wide : (k + 1) * wide] = turned(
            et_ref[...], es_ref[...], pc_ref[t], ps_ref[t]
        )
    first = dot(table[...], x)
    sign = half_sign(1, lanes)
    stack = []
    for k in range(slots):
        cos_part = first[k * wide : k * wide + block]
        sin_part = first[k * wide + block : (k + 1) * wide]
        spec = cos_part + flip_halves(sin_part) * sign
        out = dot(g_ref[0, k], spec, precision=lax.Precision.HIGHEST)
        stack += [out, flip_halves(out) * -sign]
    stack = jnp.concatenate(stack, axis=0)
    high = stack.astype(BF16)
    low_part = (stack - high.astype(F32)).astype(BF16)
    back = dot(table_t[...], high) + dot(table_t[...], low_part)
    o_ref[:, 0] = back.astype(BF16).reshape(parts, rows, lanes)


def gram(x, slots, g_t, e, et, es, rc, rs, pc, ps):
    parts, channels, rows, lanes = x.shape
    wide, line = e.shape
    count = g_t.shape[1]

    def fixed(a):
        return pl.BlockSpec(a.shape, lambda i, s: (0,) * a.ndim)

    data = pl.BlockSpec((parts, 1, rows, lanes), lambda i, s: (0, i, 0, 0))
    return pl.pallas_call(
        gram_kernel,
        grid_spec=pltpu.PrefetchScalarGridSpec(
            num_scalar_prefetch=1,
            grid=(channels,),
            in_specs=[
                data,
                pl.BlockSpec((1,) + g_t.shape[1:], lambda i, s: (i, 0, 0, 0)),
                fixed(e), fixed(et), fixed(es), fixed(rc), fixed(rs), fixed(pc), fixed(ps),
            ],
            out_specs=data,
            scratch_shapes=[
                pltpu.VMEM((count * wide, line), BF16),
                pltpu.VMEM((line, count * wide), BF16),
            ],
        ),
        out_shape=jax.ShapeDtypeStruct(x.shape, BF16),
        name="gram",
    )(slots, x, g_t, e, et, es, rc, rs, pc, ps)


def synthesis_kernel(d_ref, col_ref, row_ref, o_ref, across):
    _, frames, rows, cols = d_ref.shape
    parts = cols // LANES
    for f in range(frames):
        zero = jnp.zeros((rows, LANES), BF16)
        windows = [jnp.concatenate([zero, d_ref[0, f, :, :LANES]], axis=1)]
        for j in range(1, parts):
            windows.append(d_ref[0, f, :, (j - 1) * LANES : (j + 1) * LANES])
        windows.append(jnp.concatenate([d_ref[0, f, :, cols - LANES :], zero], axis=1))
        out = dot(jnp.concatenate(windows, axis=0), col_ref[f]).astype(BF16)
        for j in range(parts + 1):
            across[f * rows : (f + 1) * rows, j * LANES : (j + 1) * LANES] = out[
                j * rows : (j + 1) * rows
            ]
    o_ref[0] = dot(row_ref[...], across[...])


def synthesize(dual, col_band, row_band):
    channels, frames, rows, cols = dual.shape
    wide = cols + LANES
    tall = row_band.shape[0]
    return pl.pallas_call(
        synthesis_kernel,
        grid=(channels,),
        in_specs=[
            pl.BlockSpec((1, frames, rows, cols), lambda c: (c, 0, 0, 0)),
            pl.BlockSpec(col_band.shape, lambda c: (0, 0, 0)),
            pl.BlockSpec(row_band.shape, lambda c: (0, 0)),
        ],
        out_specs=pl.BlockSpec((1, tall, wide), lambda c: (c, 0, 0)),
        out_shape=jax.ShapeDtypeStruct((channels, tall, wide), F32),
        scratch_shapes=[pltpu.VMEM((frames * rows, wide), BF16)],
        cost_estimate=pl.CostEstimate(
            flops=channels * frames * rows * wide * 800, bytes_accessed=dual.size * 2, transcendentals=0
        ),
        name="synthesis",
    )(dual, col_band, row_band)


def analysis_kernel(bound_ref, p_ref, d_ref, col_ref, row_ref, o_ref, cand):
    channels, _, rows, cols = d_ref.shape
    tall = p_ref.shape[1]
    parts = cols // LANES
    bound = bound_ref[pl.program_id(0)]
    total = None
    for c in range(channels):
        windows = [p_ref[c, :, j * LANES : (j + 2) * LANES] for j in range(parts)]
        out = dot(jnp.concatenate(windows, axis=0), col_ref[0]).astype(BF16)
        across = jnp.concatenate([out[j * tall : (j + 1) * tall] for j in range(parts)], axis=1)
        new = d_ref[c, 0].astype(F32) + STEP_DUAL * dot(row_ref[0], across)
        cand[c] = new
        total = new * new if total is None else total + new * new
    scale = bound / jnp.maximum(jnp.sqrt(total), bound)
    for c in range(channels):
        o_ref[c, 0] = (cand[c] * scale).astype(BF16)


def analyse(probe, dual, col_band, row_band, bounds):
    channels, frames, rows, cols = dual.shape
    block = pl.BlockSpec((channels, 1, rows, cols), lambda f: (0, f, 0, 0))
    return pl.pallas_call(
        analysis_kernel,
        grid=(frames,),
        in_specs=[
            pl.BlockSpec(memory_space=pltpu.SMEM),
            pl.BlockSpec(probe.shape, lambda f: (0, 0, 0)),
            block,
            pl.BlockSpec((1,) + col_band.shape[1:], lambda f: (f, 0, 0)),
            pl.BlockSpec((1,) + row_band.shape[1:], lambda f: (f, 0, 0)),
        ],
        out_specs=block,
        out_shape=jax.ShapeDtypeStruct(dual.shape, BF16),
        scratch_shapes=[pltpu.VMEM((channels, rows, cols), F32)],
        name="analysis",
    )(bounds, probe, dual, col_band, row_band)


def banded(taps, offset):
    count = taps.shape[1]
    out = jnp.zeros((taps.shape[0],) + offset.shape, F32)
    for tap in range(count):
        hit = jnp.asarray(offset) == tap
        out = jnp.where(hit[None], taps[:, tap][:, None, None], out)
    return out.astype(BF16)


def shift_up(x, axis):
    count = lax.axis_size(axis)
    return lax.ppermute(x, axis, [(i, i + 1) for i in range(count - 1)])


def shift_down(x, axis):
    count = lax.axis_size(axis)
    return lax.ppermute(x, axis, [(i + 1, i) for i in range(count - 1)])


def body(sky, dual, dirty, filters, thresholds, facet_rows, tile_slots, tile_count, gram_tiles):
    channels, rows, cols = sky.shape
    taps_len = filters.shape[1]
    radius = (taps_len - 1) // 2
    fou = lax.axis_size("fou")
    img = lax.axis_size("img")
    devices = img * fou
    line = cols * fou
    block = gram_tiles.shape[-1]
    slots = gram_tiles.shape[2]
    tiles = line // block
    slab = rows // fou
    width = line // devices
    axes = ("img", "fou")

    by_row, cos_turn, sin_turn = tables(line, block)
    e = jnp.asarray(by_row)
    et = jnp.asarray(np.ascontiguousarray(by_row.T))
    es = jnp.concatenate([-et[:, block:], et[:, :block]], axis=1)
    lanes = 2 * block
    pc = jnp.broadcast_to(jnp.asarray(cos_turn)[:, :, None], (tiles, tiles, lanes))
    ps = jnp.broadcast_to(jnp.asarray(sin_turn)[:, :, None], (tiles, tiles, lanes))
    rc = jnp.tile(jnp.asarray(cos_turn), (1, line // tiles))
    rs = jnp.tile(jnp.asarray(sin_turn), (1, line // tiles))

    lines = lax.all_to_all(sky.astype(BF16), "fou", split_axis=1, concat_axis=2, tiled=True)
    spread = forward(lines.reshape(channels * slab, line), et, es, pc, ps)
    spread = spread.reshape(tiles, channels, slab, lanes)
    per = block // width
    if per > 1:
        spread = spread.reshape(tiles, channels, slab, 2, per, width)
        spread = spread.transpose(0, 4, 1, 2, 3, 5).reshape(devices, channels, slab, 2 * width)
    moved = lax.all_to_all(spread, axes, split_axis=0, concat_axis=0, tiled=True)

    identity = (jnp.arange(taps_len) == radius).astype(F32)
    taps = jnp.concatenate([identity[None], filters], axis=0)
    frames = taps.shape[0]
    tall = rows + 2 * radius
    near = np.arange(2 * LANES)[:, None]
    synth_col = banded(taps, np.arange(LANES)[None, :] + LANES - near)
    synth_row = banded(taps, np.arange(tall)[:, None] - np.arange(rows)[None, :])
    synth_row = synth_row.transpose(1, 0, 2).reshape(tall, frames * rows)
    ana_col = banded(taps, near - np.arange(LANES)[None, :])
    ana_row = banded(taps, np.arange(tall)[None, :] - np.arange(rows)[:, None])
    ext = synthesize(dual, synth_col, synth_row)
    mid = ext[:, :, radius : radius + cols]
    from_left = shift_up(ext[:, :, radius + cols : cols + 2 * radius], "fou")
    from_right = shift_down(ext[:, :, :radius], "fou")
    rest = cols - radius
    mid = mid + jnp.pad(from_left, ((0, 0), (0, 0), (0, rest))) + jnp.pad(
        from_right, ((0, 0), (0, 0), (rest, 0))
    )
    from_above = shift_up(mid[:, radius + rows :], "img")
    from_below = shift_down(mid[:, :radius], "img")
    rest = rows - radius
    synthesis = (
        mid[:, radius : radius + rows]
        + jnp.pad(from_above, ((0, 0), (0, rest), (0, 0)))
        + jnp.pad(from_below, ((0, 0), (rest, 0), (0, 0)))
    )

    which = lax.axis_index("fou") * width // block
    tile_g = lax.dynamic_index_in_dim(gram_tiles, which, 1, keepdims=False).astype(F32)
    chosen = lax.dynamic_index_in_dim(tile_slots, which, 1, keepdims=False)
    used = lax.dynamic_index_in_dim(tile_count, which, 1, keepdims=False)
    in_use = jnp.arange(slots)[None, :] < used[:, None]
    tile_g = jnp.where(in_use[:, :, None, None], jnp.swapaxes(tile_g, -1, -2), 0.0)

    if slab % 16:
        x = moved.transpose(1, 0, 2, 3).reshape(1, channels, line, 2 * width)
    else:
        x = moved
    y = gram(x, chosen, tile_g, e, et, es, rc, rs, pc, ps)
    if slab % 16:
        y = y.reshape(channels, devices, slab, 2 * width).transpose(1, 0, 2, 3)
    back = lax.all_to_all(y, axes, split_axis=0, concat_axis=0, tiled=True)
    if per > 1:
        back = back.reshape(tiles, per, channels, slab, 2, width).transpose(0, 2, 3, 4, 1, 5)
    back = back.reshape(tiles, channels * slab, lanes)
    final = backward(back, et, es, pc, ps, 1.0 / float(line * line))
    gram_image = lax.all_to_all(
        final.reshape(channels, slab, line), "fou", split_axis=2, concat_axis=1, tiled=True
    ).astype(F32)

    live_rows = (jnp.arange(rows, dtype=jnp.int32) < facet_rows[0]).astype(F32)
    image_next = (
        jnp.maximum(sky - STEP_PRIMAL * (gram_image - dirty + synthesis), 0.0)
        * live_rows[None, :, None]
    )
    probe = (2.0 * image_next - sky).astype(BF16)
    probe = jnp.concatenate(
        [shift_up(probe[:, rows - radius :], "img"), probe, shift_down(probe[:, :radius], "img")],
        axis=1,
    )
    probe = jnp.concatenate(
        [
            shift_up(probe[:, :, cols - radius :], "fou"),
            probe,
            shift_down(probe[:, :, :radius], "fou"),
            jnp.zeros((channels, tall, LANES - 2 * radius), BF16),
        ],
        axis=2,
    )
    dual_next = analyse(probe, dual, ana_col, ana_row, thresholds)
    return (image_next, dual_next)


def solution(mesh):
    in_specs = (
        P(None, "img", "fou"),
        P(None, None, "img", "fou"),
        P(None, "img", "fou"),
        P(),
        P(),
        P("img"),
        P(None, "img", None),
        P(None, "img"),
        P(None, "img", None, None, None),
    )
    out_specs = (P(None, "img", "fou"), P(None, None, "img", "fou"))
    return jax.shard_map(body, mesh=mesh, in_specs=in_specs, out_specs=out_specs, check_vma=False)
```
